256 devices in a mesh: dp: 64 (over y, z_hi, x), feat: 4 (over z_lo, core).
Axes of the slice: x: 4, y: 4, z: 8 (z_hi: 4, z_lo: 2; z = z_hi * 2 + z_lo), core: 2. Of those that a mesh axis runs over, the one named last changes fastest.
Arguments:
- features: bfloat16 [16384, 16384], P('dp', 'feat'), may hold values from -6 to 6
- gate: float32 [16384], P('dp'), may hold values from 0.1 to 1
- bias: float32 [16384], P('feat'), may hold values from -3 to 3
- down_weight: bfloat16 [16384, 512], P('feat', 'dp'), may hold values from -0.046875 to 0.046875
- up_weight: bfloat16 [512, 16384], P('dp', 'feat'), may hold values from -0.25 to 0.25
- cotangent: bfloat16 [16384, 16384], P(('dp', 'feat')), may hold values from -0.75 to 0.75
Outputs:
- cross_out: bfloat16 [16384, 16384], P(('dp', 'feat'))
- grad_up: float32 [512, 16384], P('dp', 'feat')
- grad_down: float32 [16384, 512], P('feat', 'dp')
- grad_bias: float32 [16384], P('feat')
- grad_in: bfloat16 [16384, 16384], P('dp', 'feat')
The draws below stay inside these ranges and needn't reach their ends.
All inputs are finite; a program needn't handle non-finite values.
Results may differ from the reference program's by a relative error of at most 0.0049.
Values may be sent and summed in bfloat16 or wider, within the bound.
No kernel may reach another device: no remote copies, remote signals or barrier semaphores. Data moves between devices by JAX's collectives and lax.ppermute only.
A program may use at most 128 MiB of HBM per device.

```python
import math
import jax
import jax.numpy as jnp
from jax import lax

D = 16384
RANK = 512
ROWS = 256
SAMPLES = 16384
N_DP = 64


def level_of(rng, dims, split, least, top_value):
    level, own = 1.0, jax.random.fold_in(rng, 6)
    for axis_at, parts in split:
        steps = jnp.exp(jax.random.uniform(jax.random.fold_in(own, axis_at), (parts,), jnp.float32, least / len(split), top_value / len(split)))
        level = level * jnp.repeat(steps, dims[axis_at] // parts).reshape([-1 if axis == axis_at else 1 for axis in range(len(dims))])
    return level


def normal_values(stream_key, dims, deviation, limit, pieces=(), dtype=jnp.bfloat16):
    gain = level_of(stream_key, dims, pieces, -0.22, 0.18) if pieces else 1.0
    result = jax.random.normal(stream_key, dims, jnp.float32) * deviation * gain
    return jnp.minimum(jnp.maximum(result, -limit), limit).astype(dtype)


def setup_inputs(seed: int = 0) -> dict:
    streams_of = jax.random.split(jax.random.key(seed), 7)
    features = normal_values(streams_of[0], (SAMPLES, D), 1.0, 6.0, ((0, 64), (1, 4)))
    gate = jnp.clip(jnp.exp(math.log(1.0) - 2.3025851 * jax.random.uniform(streams_of[1], (SAMPLES,), jnp.float32) ** level_of(streams_of[1], (SAMPLES,), ((0, 64),), -0.2, 0.2)), 0.1, 1.0)
    bias = normal_values(streams_of[2], (D,), 0.5, 3.0, ((0, 4),), jnp.float32)
    down_weight = normal_values(streams_of[3], (D, RANK), D ** -0.5, 0.046875, ((0, 4), (1, 64)))
    up_weight = normal_values(streams_of[4], (RANK, D), RANK ** -0.5, 0.25, ((0, 64), (1, 4)))
    cotangent = normal_values(streams_of[5], (SAMPLES, D), 0.125, 0.75, ((0, 256),))
    return {"features": features, "gate": gate, "bias": bias, "down_weight": down_weight, "up_weight": up_weight, "cotangent": cotangent}


def reference(features, gate, bias, down_weight, up_weight, cotangent):
    feat_blocks = features.reshape(N_DP, ROWS, D)
    gate_blocks = gate.reshape(N_DP, ROWS)
    cot_blocks = cotangent.reshape(N_DP, ROWS, D)

    def one_group(carry, block):
        acc_up, acc_down, acc_bias = carry
        xin, gates, cot = block
        h = jnp.dot(xin, down_weight, preferred_element_type=jnp.float32)
        low = h.astype(jnp.bfloat16)
        proj = jnp.dot(low, up_weight, preferred_element_type=jnp.float32)
        scale = gates[:, None] * proj + bias[None, :]
        xf = xin.astype(jnp.float32)
        cross = (xf * (1.0 + scale)).astype(jnp.bfloat16)
        dy = cot.astype(jnp.float32)
        pre_grad = dy * xf
        acc_bias = acc_bias + jnp.sum(pre_grad, axis=0)
        gated_grad = (gates[:, None] * pre_grad).astype(jnp.bfloat16)
        acc_up = acc_up + jnp.dot(low.T, gated_grad, preferred_element_type=jnp.float32)
        rank_grad = jnp.dot(gated_grad, up_weight.T, preferred_element_type=jnp.float32)
        low_grad = rank_grad.astype(jnp.bfloat16)
        acc_down = acc_down + jnp.dot(xin.T, low_grad, preferred_element_type=jnp.float32)
        back = jnp.dot(low_grad, down_weight.T, preferred_element_type=jnp.float32)
        grad_in = (dy * (1.0 + scale) + back).astype(jnp.bfloat16)
        return (acc_up, acc_down, acc_bias), (cross, grad_in)

    start = (jnp.zeros((RANK, D), jnp.float32), jnp.zeros((D, RANK), jnp.float32), jnp.zeros((D,), jnp.float32))
    (grad_up, grad_down, grad_bias), (cross, grad_in) = lax.scan(one_group, start, (feat_blocks, gate_blocks, cot_blocks))
    return cross.reshape(SAMPLES, D), grad_up, grad_down, grad_bias, grad_in.reshape(SAMPLES, D)
```

```python
import jax
import jax.numpy as jnp
from jax import lax
from jax.sharding import PartitionSpec as P


RING = 4
F32, BF16 = jnp.float32, jnp.bfloat16


def moved(device, axis, step):
    y, z, x = device // 16, device // 4 % 4, device % 4
    y, z, x = y + step * (axis == "y"), z + step * (axis == "z"), x + step * (axis == "x")
    return y % 4 * 16 + z % 4 * 4 + x % 4


def from_further(value, axis, step):
    return lax.ppermute(value, "dp", [(moved(i, axis, step), i) for i in range(64)])


def swap(value, bits):
    return lax.ppermute(value, "feat", [(i ^ bits, i) for i in range(4)])


def near_blocks(block, axis):
    return [block] + [from_further(block, axis, k) for k in (1, 2, 3)]


def ring_blocks(block, axis):
    half = block.shape[0] // 2
    one, three = from_further(block, axis, 1), from_further(block, axis, -1)
    low = from_further(one[:half], axis, 1)
    high = from_further(three[half:], axis, -1)
    return [block, one, jnp.concatenate([low, high], axis=0), three]


def gather(down, up):
    rank, width = up.shape
    half = width // 2
    both = jnp.stack([down.T, up])
    both = jnp.stack(near_blocks(both, "z"), axis=1).reshape(2, 4 * rank, width)
    first = jnp.stack(near_blocks(both[:, :, :half], "y"), axis=1)
    second = jnp.stack(near_blocks(both[:, :, half:], "x"), axis=1)
    full = []
    for k in range(2):
        a = ring_blocks(first[k].reshape(16 * rank, half), "x")
        b = ring_blocks(second[k].reshape(16 * rank, half), "y")
        a = jnp.concatenate(a, axis=0)
        b = jnp.stack([p.reshape(4, 4 * rank, half) for p in b], axis=1)
        full.append((a, b.reshape(64 * rank, half)))
    return full


def add(*terms):
    total = terms[0].astype(F32)
    for t in terms[1:]:
        total = total + t.astype(F32)
    return total


def ring_sum(blocks, axis):
    (l0, h0), (l1, h1), (l2, h2), (l3, h3) = blocks
    right = from_further(jnp.stack([h1, l2]), axis, -1)
    left = from_further(jnp.stack([h2, l3]), axis, 1)
    low = from_further(add(l1, right[1]).astype(BF16), axis, -1)
    high = from_further(add(h3, left[0]).astype(BF16), axis, 1)
    return add(l0, left[1], low), add(h0, right[0], high)


def near_sum(blocks, axis):
    sent = [from_further(blocks[k].astype(BF16), axis, -k) for k in (1, 2, 3)]
    return add(blocks[0], *sent)


def scatter_sum(first, second):
    rank, half = first.shape[0] // 64, first.shape[1]
    a = first.reshape(4, 2, 2, 4 * rank, half)
    b = second.reshape(2, 2, 4, 4 * rank, half)
    a = ring_sum([(a[k, 0], a[k, 1]) for k in range(4)], "x")
    b = ring_sum([(b[0, :, k], b[1, :, k]) for k in range(4)], "y")
    a = [p[k] for p in a for k in range(2)]
    b = [p[k] for p in b for k in range(2)]
    a, b = near_sum(a, "y"), near_sum(b, "x")
    both = jnp.concatenate([a, b], axis=1).reshape(4, rank, 2 * half)
    return near_sum([both[k] for k in range(4)], "z")


def rank_total(partial_value):
    rows = partial_value.shape[0] // 2
    core = lax.axis_index("feat") % 2
    mine = lax.dynamic_slice_in_dim(partial_value, core * rows, rows, 0)
    other = lax.dynamic_slice_in_dim(partial_value, (1 - core) * rows, rows, 0)
    mine = mine + swap(other, 1)
    mine = (mine + swap(mine, 2)).astype(BF16)
    other = swap(mine, 1)
    top = jnp.where(core == 0, mine, other)
    bottom = jnp.where(core == 0, other, mine)
    return jnp.concatenate([top, bottom], axis=0)


def to_features(array):
    rows, width = array.shape[0], array.shape[1] // 4
    me = lax.axis_index("feat")
    out = jnp.zeros((4 * rows, width), array.dtype)
    for k in range(4):
        piece = lax.dynamic_slice_in_dim(array, (me ^ k) * width, width, 1)
        piece = swap(piece, k) if k else piece
        out = lax.dynamic_update_slice_in_dim(out, piece, (me ^ k) * rows, 0)
    return out


def to_samples(array):
    rows, width = array.shape[0] // 4, array.shape[1]
    me = lax.axis_index("feat")
    out = jnp.zeros((rows, 4 * width), array.dtype)
    for k in range(4):
        piece = lax.dynamic_slice_in_dim(array, (me ^ k) * rows, rows, 0)
        piece = swap(piece, k) if k else piece
        out = lax.dynamic_update_slice_in_dim(out, piece, (me ^ k) * width, 1)
    return out


def everywhere_sum(value):
    for axis in "xyz":
        value = add(*near_blocks(value, axis))
    return value


def dot(a, b, ca, cb, out=F32):
    return lax.dot_general(a, b, (((ca,), (cb,)), ((), ())), preferred_element_type=F32).astype(out)


def on_device(features, gate, bias, down_weight, up_weight, cotangent):
    half = features.shape[1] // 2
    (down_a, down_b), (up_a, up_b) = gather(down_weight, up_weight)
    upstream = to_features(cotangent).astype(F32)
    xfloat = features.astype(F32)
    pre_grad = upstream * xfloat
    grad_bias = everywhere_sum(jnp.sum(pre_grad, axis=0).reshape(8, -1)).reshape(-1)
    gated_grad = (gate[:, None] * pre_grad).astype(BF16)

    low = rank_total(
        dot(features[:, :half], down_a, 1, 1) + dot(features[:, half:], down_b, 1, 1)
    )
    up_a_terms = dot(low, gated_grad[:, :half], 0, 0, BF16)
    up_b_terms = dot(low, gated_grad[:, half:], 0, 0, BF16)
    grad_up = scatter_sum(up_a_terms, up_b_terms)

    low_grad = rank_total(
        dot(gated_grad[:, :half], up_a, 1, 1) + dot(gated_grad[:, half:], up_b, 1, 1)
    )
    down_a_terms = dot(low_grad, features[:, :half], 0, 0, BF16)
    down_b_terms = dot(low_grad, features[:, half:], 0, 0, BF16)
    grad_down = scatter_sum(down_a_terms, down_b_terms).T

    proj = jnp.concatenate([dot(low, up_a, 1, 0), dot(low, up_b, 1, 0)], axis=1)
    scale = gate[:, None] * proj + bias[None, :]
    cross_out = to_samples((xfloat * (1.0 + scale)).astype(BF16))
    back = jnp.concatenate([dot(low_grad, down_a, 1, 0), dot(low_grad, down_b, 1, 0)], axis=1)
    grad_in = (upstream * (1.0 + scale) + back).astype(BF16)
    return (cross_out, grad_up, grad_down, grad_bias, grad_in)


def solution(mesh):
    in_specs = (
        P("dp", "feat"),
        P("dp"),
        P("feat"),
        P("feat", "dp"),
        P("dp", "feat"),
        P(("dp", "feat"), None),
    )
    out_specs = (
        P(("dp", "feat"), None),
        P("dp", "feat"),
        P("feat", "dp"),
        P("feat"),
        P("dp", "feat"),
    )
    return jax.shard_map(
        on_device, mesh=mesh, in_specs=in_specs, out_specs=out_specs, check_vma=False
    )
```

```python
import jax
import jax.numpy as jnp
from jax import lax
from jax.sharding import PartitionSpec as P


F32, BF16 = jnp.float32, jnp.bfloat16

BITS = {"y": 4, "z": 2, "x": 0}


def swap(value, axis, bits):
    return lax.ppermute(value, "dp", [(i ^ bits << BITS[axis], i) for i in range(64)])


def feat_swap(value, bits):
    return lax.ppermute(value, "feat", [(i ^ bits, i) for i in range(4)])


def cat(*pieces):
    return jnp.concatenate(pieces, axis=0)


def near_blocks(block, axis):
    got = {k: swap(block, axis, k) for k in (1, 3, 2)}
    return [block, got[1], got[2], got[3]]


def ring_blocks(block, axis):
    one = swap(block, axis, 1)
    three = swap(block, axis, 3)
    down = swap(three[0], axis, 1)
    up = swap(one[1], axis, 3)
    return [block[0], one[0], down, three[0]], [block[1], one[1], up, three[1]]


def gather(down, up):
    rank, width = up.shape
    half = width // 2
    near = jnp.stack(near_blocks(jnp.stack([down.T, up]), "z"), axis=1)
    near = near.reshape(2, 4 * rank, width)
    a = jnp.stack(near_blocks(near[:, :, :half], "y"), axis=1)
    b = jnp.stack(near_blocks(near[:, :, half:], "x"), axis=1)
    a = ring_blocks(a.reshape(2, 16 * rank, half), "x")
    b = ring_blocks(b.reshape(2, 16 * rank, half), "y")
    return [(a[k], b[k]) for k in range(2)]


def assembled(blocks):
    a, b = blocks
    rows, width = b[0].shape
    turned = jnp.stack([p.reshape(4, rows // 4, width) for p in b], axis=1)
    return cat(*a), turned.reshape(4 * rows, width)


def add(*terms):
    total = terms[0].astype(F32)
    for t in terms[1:]:
        total = total + t.astype(F32)
    return total


def pack(vector, width):
    if vector is None:
        return []
    high = lax.reduce_precision(vector, 8, 7)
    parts = cat(high, vector - high).astype(BF16).reshape(-1, width)
    return [jnp.pad(parts, ((0, 8 - parts.shape[0]), (0, 0)))]


def unpack(vector, *riders):
    if vector is None:
        return None
    n = vector.size
    for r in riders:
        r = r.astype(F32).reshape(-1)
        vector = vector + r[:n] + r[n : 2 * n]
    return vector


def near_sum(blocks, axis, rider=None):
    rows, width = blocks[0].shape
    extra = pack(rider, width)
    got = [swap(cat(blocks[k].astype(BF16), *extra), axis, k) for k in (1, 3, 2)]
    total = add(blocks[0], *(g[:rows] for g in got))
    return total, unpack(rider, *(g[rows:] for g in got))


def two_step_sum(blocks, axis, first, rider=None):
    rows, width = blocks[0].shape
    other = first ^ 2
    near, far = blocks[first], blocks[2]
    sent = cat(*((near, far) if first == 1 else (far, near)), *pack(rider, width))
    got = swap(sent, axis, first)
    near, far = (0, rows) if first == 1 else (rows, 0)
    rider = unpack(rider, got[2 * rows :])
    passed = add(blocks[other], got[far : far + rows]).astype(BF16)
    passed, got = lax.optimization_barrier((passed, got))
    last = swap(cat(passed, *pack(rider, width)), axis, other)
    total = add(blocks[0], got[near : near + rows], last[:rows])
    return total, unpack(rider, last[rows:]), sent


def blocks_of(terms):
    rows = terms.shape[0] // 4
    return [terms[k * rows : (k + 1) * rows] for k in range(4)]


def turned_blocks_of(terms):
    rows, width = terms.shape
    terms = terms.reshape(4, 4, rows // 16, width)
    return [terms[:, k].reshape(rows // 4, width) for k in range(4)]


def rank_totals(first, second):
    rows = first.shape[0] // 2
    core = lax.axis_index("feat") & 1

    def part(k):
        return cat(*(lax.dynamic_slice_in_dim(p, k * rows, rows, 0) for p in (first, second)))

    mine = part(core) + feat_swap(part(1 - core), 1)
    mine = add(mine, feat_swap(mine.astype(BF16), 2)).astype(BF16)
    other = feat_swap(mine, 1)
    top = jnp.where(core == 0, mine, other)
    bottom = jnp.where(core == 0, other, mine)
    return cat(top[:rows], bottom[:rows]), cat(top[rows:], bottom[rows:])


def to_features(array):
    rows, width = array.shape[0], array.shape[1] // 4
    me = lax.axis_index("feat")
    pieces = [lax.dynamic_slice_in_dim(array, (me ^ k) * width, width, 1) for k in range(4)]
    pieces = [feat_swap(p, k) if k else p for k, p in enumerate(pieces)]
    out = jnp.zeros((4 * rows, width), array.dtype)
    for k, piece in enumerate(pieces):
        out = lax.dynamic_update_slice_in_dim(out, piece, (me ^ k) * rows, 0)
    return out


def to_samples(array):
    rows = array.shape[0] // 4
    me = lax.axis_index("feat")
    pieces = [lax.dynamic_slice_in_dim(array, (me ^ k) * rows, rows, 0) for k in range(4)]
    return [feat_swap(p, k) if k else p for k, p in enumerate(pieces)]


def side_by_side(pieces):
    rows, width = pieces[0].shape
    me = lax.axis_index("feat")
    out = jnp.zeros((rows, 4 * width), pieces[0].dtype)
    for k, piece in enumerate(pieces):
        out = lax.dynamic_update_slice_in_dim(out, piece, (me ^ k) * width, 1)
    return out


def dot(a, b, ca, cb, out=F32):
    return lax.dot_general(a, b, (((ca,), (cb,)), ((), ())), preferred_element_type=F32).astype(out)


def work(features, gate, bias, down_weight, up_weight, cotangent):
    rank, half = up_weight.shape[0], features.shape[1] // 2
    down_blocks, up_blocks = gather(down_weight, up_weight)
    (down_a, down_b), (up_a, up_b) = assembled(down_blocks), assembled(up_blocks)
    upstream = to_features(cotangent).astype(F32)
    xfloat = features.astype(F32)
    pre_grad = upstream * xfloat
    rider = jnp.sum(pre_grad, axis=0)
    gated_grad = (gate[:, None] * pre_grad).astype(BF16)

    low, low_grad = rank_totals(
        dot(features[:, :half], down_a, 1, 1) + dot(features[:, half:], down_b, 1, 1),
        dot(gated_grad[:, :half], up_a, 1, 1) + dot(gated_grad[:, half:], up_b, 1, 1),
    )
    a_up = blocks_of(dot(low, gated_grad[:, :half], 0, 0, BF16))
    b_up = turned_blocks_of(dot(low, gated_grad[:, half:], 0, 0, BF16))
    a_up, rider, a_sent = two_step_sum(a_up, "x", 1, rider)
    b_up, _, b_sent = two_step_sum(b_up, "y", 1)
    low_grad, _ = lax.optimization_barrier((low_grad, (a_sent, b_sent)))
    a_down = blocks_of(dot(low_grad, features[:, :half], 0, 0, BF16))
    b_down = turned_blocks_of(dot(low_grad, features[:, half:], 0, 0, BF16))
    a_down, _, _ = two_step_sum(a_down, "x", 3)
    b_down, _, _ = two_step_sum(b_down, "y", 3)

    def joined(up, down):
        return [cat(u, d) for u, d in zip(blocks_of(up), blocks_of(down))]

    a, rider = near_sum(joined(a_up, a_down), "y", rider)
    b, _ = near_sum(joined(b_up, b_down), "x")

    proj = jnp.concatenate([dot(low, up_a, 1, 0), dot(low, up_b, 1, 0)], axis=1)
    scale = gate[:, None] * proj + bias[None, :]
    pieces = to_samples((xfloat * (1.0 + scale)).astype(BF16))
    pieces, a = lax.optimization_barrier((pieces, a))
    cross_out = side_by_side(pieces)
    back = jnp.concatenate([dot(low_grad, down_a, 1, 0), dot(low_grad, down_b, 1, 0)], axis=1)
    grad_in = (upstream * (1.0 + scale) + back).astype(BF16)

    rider = rider + swap(rider, "z", 1)
    grad_bias = rider + swap(rider, "z", 3)
    both = jnp.concatenate([a, b], axis=1).reshape(2, 4, rank, 2 * half)
    both = [both[:, k].reshape(2 * rank, 2 * half) for k in range(4)]
    both, _ = near_sum(both, "z")
    return (cross_out, both[:rank], both[rank:].T, grad_bias, grad_in)


def solution(mesh):
    in_specs = (
        P("dp", "feat"),
        P("dp"),
        P("feat"),
        P("feat", "dp"),
        P("dp", "feat"),
        P(("dp", "feat"), None),
    )
    out_specs = (
        P(("dp", "feat"), None),
        P("dp", "feat"),
        P("feat", "dp"),
        P("feat"),
        P("dp", "feat"),
    )
    return jax.shard_map(work, mesh=mesh, in_specs=in_specs, out_specs=out_specs, check_vma=False)
```

```python
import jax
import jax.numpy as jnp
from jax import lax
from jax.sharding import PartitionSpec as P


F32, BF16 = jnp.float32, jnp.bfloat16

BITS = {"y": 4, "z": 2, "x": 0}


def swap(value, axis, bits):
    return lax.ppermute(value, "dp", [(i ^ bits << BITS[axis], i) for i in range(64)])


def feat_swap(value, bits):
    return lax.ppermute(value, "feat", [(i ^ bits, i) for i in range(4)])


def cat(*pieces):
    return jnp.concatenate(pieces, axis=0)


def near_blocks(block, axis):
    got = {k: swap(block, axis, k) for k in (1, 3, 2)}
    return [block, got[1], got[2], got[3]]


def ring_blocks(block, axis):
    one = swap(block, axis, 1)
    three = swap(block, axis, 3)
    down = swap(three[0], axis, 1)
    up = swap(one[1], axis, 3)
    return [block[0], one[0], down, three[0]], [block[1], one[1], up, three[1]]


def gather(down, up):
    rank, width = up.shape
    half = width // 2
    near = jnp.stack(near_blocks(jnp.stack([down.T, up]), "z"), axis=1)
    near = near.reshape(2, 4 * rank, width)
    a = jnp.stack(near_blocks(near[:, :, :half], "y"), axis=1)
    b = jnp.stack(near_blocks(near[:, :, half:], "x"), axis=1)
    a = ring_blocks(a.reshape(2, 16 * rank, half), "x")
    b = ring_blocks(b.reshape(2, 16 * rank, half), "y")
    return [(a[k], b[k]) for k in range(2)]


def assembled(blocks):
    a, b = blocks
    rows, width = b[0].shape
    turned = jnp.stack([p.reshape(4, rows // 4, width) for p in b], axis=1)
    return cat(*a), turned.reshape(4 * rows, width)


def add(*terms):
    total = terms[0].astype(F32)
    for t in terms[1:]:
        total = total + t.astype(F32)
    return total


def pack(vector, width):
    if vector is None:
        return []
    high = lax.reduce_precision(vector, 8, 7)
    parts = cat(high, vector - high).astype(BF16).reshape(-1, width)
    return [jnp.pad(parts, ((0, 8 - parts.shape[0]), (0, 0)))]


def unpack(vector, *riders):
    if vector is None:
        return None
    n = vector.size
    for r in riders:
        r = r.astype(F32).reshape(-1)
        vector = vector + r[:n] + r[n : 2 * n]
    return vector


def near_sum(blocks, axis, rider=None):
    rows, width = blocks[0].shape
    extra = pack(rider, width)
    got = [swap(cat(blocks[k].astype(BF16), *extra), axis, k) for k in (1, 3, 2)]
    total = add(blocks[0], *(g[:rows] for g in got))
    return total, unpack(rider, *(g[rows:] for g in got))


def two_step_sum(blocks, axis, first, rider=None):
    rows, width = blocks[0].shape
    other = first ^ 2
    near, far = blocks[first], blocks[2]
    sent = cat(*((near, far) if first == 1 else (far, near)), *pack(rider, width))
    got = swap(sent, axis, first)
    near, far = (0, rows) if first == 1 else (rows, 0)
    rider = unpack(rider, got[2 * rows :])
    passed = add(blocks[other], got[far : far + rows]).astype(BF16)
    passed, got = lax.optimization_barrier((passed, got))
    last = swap(cat(passed, *pack(rider, width)), axis, other)
    total = add(blocks[0], got[near : near + rows], last[:rows])
    return total, unpack(rider, last[rows:]), sent


def blocks_of(terms):
    rows = terms.shape[0] // 4
    return [terms[k * rows : (k + 1) * rows] for k in range(4)]


def turned_blocks_of(terms):
    rows, width = terms.shape
    terms = terms.reshape(4, 4, rows // 16, width)
    return [terms[:, k].reshape(rows // 4, width) for k in range(4)]


def rank_totals(first, second):
    rows = first.shape[0] // 2
    core = lax.axis_index("feat") & 1

    def part(k):
        return cat(*(lax.dynamic_slice_in_dim(p, k * rows, rows, 0) for p in (first, second)))

    mine = part(core) + feat_swap(part(1 - core), 1)
    mine = add(mine, feat_swap(mine.astype(BF16), 2)).astype(BF16)
    other = feat_swap(mine, 1)
    top = jnp.where(core == 0, mine, other)
    bottom = jnp.where(core == 0, other, mine)
    return cat(top[:rows], bottom[:rows]), cat(top[rows:], bottom[rows:])


def to_features(array):
    rows, width = array.shape[0], array.shape[1] // 4
    me = lax.axis_index("feat")
    pieces = [lax.dynamic_slice_in_dim(array, (me ^ k) * width, width, 1) for k in range(4)]
    pieces = [feat_swap(p, k) if k else p for k, p in enumerate(pieces)]
    out = jnp.zeros((4 * rows, width), array.dtype)
    for k, piece in enumerate(pieces):
        out = lax.dynamic_update_slice_in_dim(out, piece, (me ^ k) * rows, 0)
    return out


def to_samples(array):
    rows = array.shape[0] // 4
    me = lax.axis_index("feat")
    pieces = [lax.dynamic_slice_in_dim(array, (me ^ k) * rows, rows, 0) for k in range(4)]
    return [feat_swap(p, k) if k else p for k, p in enumerate(pieces)]


def side_by_side(pieces):
    rows, width = pieces[0].shape
    me = lax.axis_index("feat")
    out = jnp.zeros((rows, 4 * width), pieces[0].dtype)
    for k, piece in enumerate(pieces):
        out = lax.dynamic_update_slice_in_dim(out, piece, (me ^ k) * width, 1)
    return out


def dot(a, b, ca, cb, out=F32):
    return lax.dot_general(a, b, (((ca,), (cb,)), ((), ())), preferred_element_type=F32).astype(out)


def work(features, gate, bias, down_weight, up_weight, cotangent):
    rank, half = up_weight.shape[0], features.shape[1] // 2
    down_blocks, up_blocks = gather(down_weight, up_weight)
    (down_a, down_b), (up_a, up_b) = assembled(down_blocks), assembled(up_blocks)
    upstream = to_features(cotangent).astype(F32)
    xfloat = features.astype(F32)
    pre_grad = upstream * xfloat
    rider = jnp.sum(pre_grad, axis=0)
    gated_grad = (gate[:, None] * pre_grad).astype(BF16)

    low, low_grad = rank_totals(
        dot(features[:, :half], down_a, 1, 1) + dot(features[:, half:], down_b, 1, 1),
        dot(gated_grad[:, :half], up_a, 1, 1) + dot(gated_grad[:, half:], up_b, 1, 1),
    )
    up = dot(low, gated_grad, 0, 0, BF16)
    a_up, b_up = blocks_of(up[:, :half]), turned_blocks_of(up[:, half:])
    a_up, rider, a_sent = two_step_sum(a_up, "x", 1, rider)
    b_up, _, b_sent = two_step_sum(b_up, "y", 1)
    low_grad, _ = lax.optimization_barrier((low_grad, (a_sent, b_sent)))
    down = dot(low_grad, features, 0, 0, BF16)
    a_down, b_down = blocks_of(down[:, :half]), turned_blocks_of(down[:, half:])
    a_down, _, _ = two_step_sum(a_down, "x", 3)
    b_down, _, _ = two_step_sum(b_down, "y", 3)

    def joined(up, down):
        return [cat(u, d) for u, d in zip(blocks_of(up), blocks_of(down))]

    a, rider = near_sum(joined(a_up, a_down), "y", rider)
    b, _ = near_sum(joined(b_up, b_down), "x")

    proj = jnp.concatenate([dot(low, up_a, 1, 0), dot(low, up_b, 1, 0)], axis=1)
    scale = gate[:, None] * proj + bias[None, :]
    pieces = to_samples((xfloat * (1.0 + scale)).astype(BF16))
    pieces, a = lax.optimization_barrier((pieces, a))
    cross_out = side_by_side(pieces)
    back = jnp.concatenate([dot(low_grad, down_a, 1, 0), dot(low_grad, down_b, 1, 0)], axis=1)
    grad_in = (upstream * (1.0 + scale) + back).astype(BF16)

    rider = rider + swap(rider, "z", 1)
    grad_bias = rider + swap(rider, "z", 3)
    both = jnp.concatenate([a, b], axis=1).reshape(2, 4, rank, 2 * half)
    both = [both[:, k].reshape(2 * rank, 2 * half) for k in range(4)]
    both, _ = near_sum(both, "z")
    return (cross_out, both[:rank], both[rank:].T, grad_bias, grad_in)


def solution(mesh):
    in_specs = (
        P("dp", "feat"),
        P("dp"),
        P("feat"),
        P("feat", "dp"),
        P("dp", "feat"),
        P(("dp", "feat"), None),
    )
    out_specs = (
        P(("dp", "feat"), None),
        P("dp", "feat"),
        P("feat", "dp"),
        P("feat"),
        P("dp", "feat"),
    )
    return jax.shard_map(work, mesh=mesh, in_specs=in_specs, out_specs=out_specs, check_vma=False)
```
